1024 devices in a mesh: seq: 128 (over y, z), head: 8 (over x, core).
Axes of the slice: x: 4, y: 8, z: 16, core: 2. Of those that a mesh axis runs over, the one named last changes fastest.
Arguments:
- query_rows: bfloat16 [16384, 4096], P('seq', 'head'), may hold values from -6 to 6
- key_rows: bfloat16 [16384, 4096], P('seq', 'head'), may hold values from -6 to 6
- value_rows: bfloat16 [16384, 4096], P('seq', 'head'), may hold values from -70 to 70
- log_decay: float32 [32, 16384], P('head', 'seq'), may hold values from -1.6 to 0
- cotangent: bfloat16 [16384, 4096], P('seq', 'head'), may hold values from -6 to 6
Outputs:
- attended: bfloat16 [16384, 4096], P('seq', 'head')
- query_grad: bfloat16 [16384, 4096], P('seq', 'head')
- key_grad: bfloat16 [16384, 4096], P('seq', 'head')
- value_grad: bfloat16 [16384, 4096], P('seq', 'head')
The draws below stay inside these ranges and needn't reach their ends.
All inputs are finite; a program needn't handle non-finite values.
Results may differ from the reference program's by a relative error of at most 0.0054.
Values sent between devices are 32-bit elements; how exact they have to be, the bound alone decides.
A program may use at most 128 MiB of HBM per device.

```python
import math
import jax
import jax.numpy as jnp
from jax import lax

DH = 128
TOK_DEV = 128
HEADS = 32
TOKENS = 16384
BLOCKS = 128
WIDTH = 4096


def draw_log_decay(key, part):
    streams = jax.random.split(key, 7)
    fast_share = 0.5
    is_fast = jax.random.uniform(streams[0], (HEADS, 1)) < fast_share
    slow_rate = jnp.exp(jax.random.uniform(streams[1], (HEADS, 1), minval=math.log(0.1), maxval=math.log(0.6))) / TOKENS
    fast_rate = jnp.exp(jax.random.uniform(streams[2], (HEADS, 1), minval=math.log(1.0 / 50.0), maxval=math.log(1.0 / 30.0)))
    reference_fading_speed = jnp.where(is_fast, fast_rate, slow_rate)
    segment_attenuation_multiplier = jnp.exp(jax.random.uniform(streams[3], (HEADS, BLOCKS, 1), minval=-math.log(2.0), maxval=math.log(2.0)))
    segment_attenuation_multiplier = jnp.broadcast_to(segment_attenuation_multiplier, (HEADS, BLOCKS, TOK_DEV)).reshape(HEADS, TOKENS)
    element_attenuation_multiplier = jax.random.uniform(streams[4], (HEADS, TOKENS), minval=0.5, maxval=1.5)
    element_offsets = jax.random.randint(streams[5], (HEADS, 2), 0, TOKENS)
    network_level_indices = jax.random.uniform(streams[6], (HEADS, 2), minval=math.log(0.5), maxval=math.log(0.8))
    element_indices = jnp.arange(TOKENS)
    segment_count = jnp.sum(jnp.where(element_indices[None, :, None] == element_offsets[:, None, :], network_level_indices[:, None, :], 0.0), axis=2)
    return (segment_count - reference_fading_speed * segment_attenuation_multiplier * element_attenuation_multiplier).astype(jnp.float32)


def draw_value_rows(key, part):
    streams = jax.random.split(key, 1)
    column_head = (jnp.arange(WIDTH) // DH).astype(jnp.float32)
    head_scale = 10.0 ** (column_head / (HEADS - 1))
    base = jnp.clip(jax.random.normal(streams[0], (TOKENS, WIDTH)), -4.0, 4.0)
    result = base * head_scale[None, :]
    return result.astype(jnp.float32).astype(jnp.bfloat16)


def block_scale(own_key, extent, cuts, smallest, top_value):
    def one(position, shards_of):
        draws = jax.random.uniform(jax.random.fold_in(jax.random.fold_in(own_key, 6), position), (shards_of,), jnp.float32, smallest / len(cuts), top_value / len(cuts))
        return jnp.repeat(jnp.exp(draws), extent[position] // shards_of).reshape((-1,) + (1,) * (len(extent) - position - 1))

    level = one(*cuts[0])
    for cut in cuts[1:]:
        level = level * one(*cut)
    return level


def scatter_about(rng, shape, width, bound, cuts=(), kind=jnp.bfloat16):
    values = jax.random.normal(rng, shape, jnp.float32) * width
    if len(cuts) > 0:
        values = block_scale(rng, shape, cuts, -0.22, 0.18) * values
    return jnp.clip(values, min=-bound, max=bound).astype(kind)


def setup_inputs(seed: int = 0) -> dict:
    key_list = jax.random.split(jax.random.key(seed), 6)
    return {
        "query_rows": scatter_about(key_list[0], (TOKENS, WIDTH), 1.0, 6.0, ((0, 128), (1, 8))),
        "key_rows": scatter_about(key_list[1], (TOKENS, WIDTH), 1.0, 6.0, ((0, 128), (1, 8))),
        "value_rows": draw_value_rows(jax.random.fold_in(key_list[5], 71), 0),
        "log_decay": draw_log_decay(jax.random.fold_in(key_list[5], 71), 0),
        "cotangent": scatter_about(key_list[4], (TOKENS, WIDTH), 1.0, 6.0, ((0, 128), (1, 8))),
    }


highest = lax.Precision.HIGHEST

def to_blocks(matrix):
    return matrix.reshape(BLOCKS, TOK_DEV, HEADS, DH).transpose(0, 2, 1, 3)

def from_blocks(stack):
    return stack.transpose(0, 2, 1, 3).reshape(TOKENS, WIDTH)

def block_terms(query_blk, key_blk, decay_blk):
    causal = jnp.tril(jnp.ones((TOK_DEV, TOK_DEV), dtype=bool))
    cumulative = jnp.cumsum(decay_blk, axis=-1)
    totals = cumulative[:, -1]
    spread = cumulative[:, :, None] - cumulative[:, None, :]
    decay_matrix = jnp.where(causal[None], jnp.exp(jnp.minimum(spread, 0.0)), 0.0)
    query_float = query_blk.astype(jnp.float32)
    key_float = key_blk.astype(jnp.float32)
    scores = jnp.einsum('htd,hsd->hts', query_float, key_float)
    weights = (scores * decay_matrix).astype(jnp.bfloat16)
    scaled_queries = query_float * jnp.exp(cumulative)[..., None]
    fade_out = jnp.exp(totals[:, None] - cumulative)[..., None]
    return (cumulative, totals, decay_matrix, weights, scaled_queries, fade_out)

def reference(query_rows, key_rows, value_rows, log_decay, cotangent):
    queries = to_blocks(query_rows)
    key_blocks = to_blocks(key_rows)
    value_blocks = to_blocks(value_rows)
    decays = log_decay.reshape(HEADS, BLOCKS, TOK_DEV).transpose(1, 0, 2)

    def forward_step(state, inputs):
        query_blk, key_blk, value_blk, decay_blk = inputs
        cumulative, totals, decay_matrix, weights, scaled_queries, fade_out = block_terms(query_blk, key_blk, decay_blk)
        value_float = value_blk.astype(jnp.float32)
        raw = jnp.einsum('htd,hde->hte', scaled_queries, state, precision=highest)
        raw = raw + jnp.einsum('hts,hse->hte', weights.astype(jnp.float32), value_float)
        scaled_keys = (key_blk.astype(jnp.float32) * fade_out).astype(jnp.bfloat16)
        block_state = jnp.einsum('htd,hte->hde', scaled_keys.astype(jnp.float32), value_float)
        new_state = jnp.exp(totals)[:, None, None] * state + block_state
        return (new_state, (raw, state))
    start = jnp.zeros((HEADS, DH, DH), jnp.float32)
    _, (raw_blocks, states_in) = lax.scan(forward_step, start, (queries, key_blocks, value_blocks, decays))
    raw = from_blocks(raw_blocks)
    inverse_norm = lax.rsqrt(lax.optimization_barrier(jnp.mean(raw * raw, axis=1, keepdims=True)) + 1e-06)
    normed = raw * inverse_norm
    attended = normed.astype(jnp.bfloat16)
    upstream = cotangent.astype(jnp.float32)
    mean_dot = lax.optimization_barrier(jnp.mean(upstream * normed, axis=1, keepdims=True))
    raw_grad = (inverse_norm * (upstream - normed * mean_dot)).astype(jnp.bfloat16)
    grad_blocks = to_blocks(raw_grad)

    def backward_step(grad_state, inputs):
        query_blk, key_blk, value_blk, decay_blk, grad_blk, state_blk = inputs
        cumulative, totals, decay_matrix, weights, scaled_queries, fade_out = block_terms(query_blk, key_blk, decay_blk)
        query_float = query_blk.astype(jnp.float32)
        key_float = key_blk.astype(jnp.float32)
        value_float = value_blk.astype(jnp.float32)
        grad_float = grad_blk.astype(jnp.float32)
        grad_scores = jnp.einsum('hte,hse->hts', grad_float, value_float)
        grad_weights = (grad_scores * decay_matrix).astype(jnp.bfloat16).astype(jnp.float32)
        query_part = jnp.exp(cumulative)[..., None] * jnp.einsum('hte,hde->htd', grad_float, state_blk, precision=highest)
        query_part = query_part + jnp.einsum('hts,hsd->htd', grad_weights, key_float)
        key_part = jnp.einsum('hts,htd->hsd', grad_weights, query_float)
        key_part = key_part + fade_out * jnp.einsum('hse,hde->hsd', value_float, grad_state, precision=highest)
        value_part = jnp.einsum('hts,hte->hse', weights.astype(jnp.float32), grad_float)
        value_part = value_part + fade_out * jnp.einsum('hsd,hde->hse', key_float, grad_state, precision=highest)
        query_state = jnp.einsum('htd,hte->hde', scaled_queries, grad_float, precision=highest)
        new_grad = jnp.exp(totals)[:, None, None] * grad_state + query_state
        return (new_grad, (query_part.astype(jnp.bfloat16), key_part.astype(jnp.bfloat16), value_part.astype(jnp.bfloat16)))
    _, (query_out, key_out, value_out) = lax.scan(backward_step, start, (queries, key_blocks, value_blocks, decays, grad_blocks, states_in), reverse=True)
    return (attended, from_blocks(query_out), from_blocks(key_out), from_blocks(value_out))
```

```python
import functools

import jax
import jax.numpy as jnp
from jax import lax
from jax.experimental import pallas as pl
from jax.experimental.pallas import tpu as pltpu
from jax.sharding import PartitionSpec as P

ROW = 16
CHUNKS = 2
MESH = pl.DeviceIdType.MESH
F32 = jnp.float32
BF16 = jnp.bfloat16


def dot(a, b, dims, precision=None):
    return lax.dot_general(
        a, b, (dims, ((), ())), precision=precision, preferred_element_type=F32
    )


NN = ((1,), (0,))
NT = ((1,), (1,))
TN = ((0,), (0,))


def halves(x):
    high = x.astype(BF16)
    return high, (x - high.astype(F32)).astype(BF16)


def kernel(
    Y,
    Z,
    N,
    C,
    q_ref,
    k_ref,
    v_ref,
    ld_ref,
    ct_ref,
    att_ref,
    qg_ref,
    kg_ref,
    vg_ref,
    block,
    came,
    excl,
    state,
    tot_out,
    tot_in,
    fade_d,
    row_out,
    row_in,
    sums_out,
    sums_in,
    decay_s,
    weights_s,
    intra_s,
    raw_s,
    rg_s,
    sqt_s,
    growth_s,
    fade_s,
    in_ssem,
    in_rsem,
    out_ssem,
    out_rsem,
    y_ssem,
    y_rsem,
    t_ssem,
    t_rsem,
    x_ssem,
    x_rsem,
):
    H = ld_ref.shape[0]
    T = ld_ref.shape[1]
    D = q_ref.shape[1] // H
    rows = H * D // Z
    part = rows // C
    per_head = D // rows
    width = D * H * N
    seq = lax.axis_index("seq")
    mine = lax.axis_index("head")
    y = lax.div(seq, Z)
    z = lax.rem(seq, Z)

    barrier = pltpu.get_barrier_semaphore()

    def far_first(count, i):
        half = count // 2
        return half + jnp.where(lax.rem(i, 2) == 0, lax.div(i, 2), -lax.div(i + 1, 2))

    def peers(count, at, visit):
        def step(i, carry):
            visit(lax.rem(at + far_first(count, i), count))
            return carry

        lax.fori_loop(0, count - 1, step, 0)

    def z_device(other):
        return (y * Z + other, mine)

    def y_device(other):
        return (other * Z + z, mine)

    def x_device(other):
        return (seq, other)

    for count, at, device in ((Z, z, z_device), (Y, y, y_device), (N, mine, x_device)):

        def greet(other, device=device):
            pl.semaphore_signal(barrier, inc=1, device_id=device(other), device_id_type=MESH)

        peers(count, at, greet)

    t_i = lax.broadcasted_iota(jnp.int32, (T, T), 0)
    s_i = lax.broadcasted_iota(jnp.int32, (T, T), 1)
    causal = t_i >= s_i
    eye = t_i == s_i
    lower = causal.astype(F32)
    ld = ld_ref[...]
    cum_row = dot(ld, lower, NT, lax.Precision.HIGHEST)
    cum_col = dot(lower, ld, NT, lax.Precision.HIGHEST)
    totals = cum_row[:, T - 1 : T]

    def head(ref, h):
        return ref[:, h * D : (h + 1) * D]

    for h in range(H):
        total = totals[h : h + 1, :]
        tot_out[h] = jnp.broadcast_to(total, (1, D))
        column = cum_col[:, h : h + 1]
        fade = jnp.broadcast_to(jnp.exp(jnp.broadcast_to(total, (T, 1)) - column), (T, D))
        fade_s[h] = fade
        scaled = (head(k_ref, h).astype(F32) * fade).astype(BF16)
        block[0, h * D : (h + 1) * D, :] = dot(scaled, head(v_ref, h), TN)

    pl.semaphore_wait(barrier, (Z - 1) + (Y - 1) + (N - 1))

    def t_copy(other, src, slot):
        return pltpu.make_async_remote_copy(
            src_ref=tot_out.at[src],
            dst_ref=tot_in.at[slot],
            send_sem=t_ssem.at[other],
            recv_sem=t_rsem.at[slot],
            device_id=z_device(other),
            device_id_type=MESH,
        )

    peers(Z, z, lambda other: t_copy(other, lax.div(other, per_head), z).start())
    tot_in[z] = tot_out[lax.div(z, per_head)]

    def in_copy(w, c, other, slot):
        return pltpu.make_async_remote_copy(
            src_ref=block.at[w, pl.ds(pl.multiple_of(other * rows + c * part, part), part)],
            dst_ref=came.at[w, slot, pl.ds(c * part, part)],
            send_sem=in_ssem.at[w, c, other],
            recv_sem=in_rsem.at[w, c, slot],
            device_id=z_device(other),
            device_id_type=MESH,
        )

    def out_copy(w, c, other, slot):
        return pltpu.make_async_remote_copy(
            src_ref=excl.at[w, other, pl.ds(c * part, part)],
            dst_ref=state.at[w, pl.ds(pl.multiple_of(slot * rows + c * part, part), part)],
            send_sem=out_ssem.at[w, c, other],
            recv_sem=out_rsem.at[w, c, slot],
            device_id=z_device(other),
            device_id_type=MESH,
        )

    def y_copy(w, c, other, slot):
        return pltpu.make_async_remote_copy(
            src_ref=row_out.at[w, c],
            dst_ref=row_in.at[w, c, slot],
            send_sem=y_ssem.at[w, c, other],
            recv_sem=y_rsem.at[w, c, slot],
            device_id=y_device(other),
            device_id_type=MESH,
        )

    def x_copy(other, slot):
        return pltpu.make_async_remote_copy(
            src_ref=sums_out,
            dst_ref=sums_in.at[slot],
            send_sem=x_ssem.at[other],
            recv_sem=x_rsem.at[slot],
            device_id=x_device(other),
            device_id_type=MESH,
        )

    def enter(w):
        for c in range(C):
            peers(Z, z, lambda other: in_copy(w, c, other, z).start())
        came[w, z] = block[w, pl.ds(pl.multiple_of(z * rows, rows), rows), :]

    def scan(w):
        for c in range(C):
            peers(Z, z, lambda other: in_copy(w, c, other, other).wait_recv())
            if w == 0 and c == 0:
                peers(Z, z, lambda other: t_copy(other, 0, other).wait_recv())
            piece = slice(c * part, (c + 1) * part)

            def step(i, carry):
                total, passed = carry
                at = i if w == 0 else Z - 1 - i
                excl[w, at, piece, :] = total
                if c == 0:
                    fade_d[w, at] = passed
                one = tot_in[at]
                total = jnp.exp(one) * total + came[w, at, piece, :]
                return total, passed + one

            total, passed = lax.fori_loop(
                0, Z, step, (jnp.zeros((part, D), F32), jnp.zeros((1, D), F32)), unroll=4
            )
            row_out[w, c, 0:part, :] = total
            row_out[w, c, part : part + 8, :] = jnp.broadcast_to(passed, (8, D))
            peers(Y, y, lambda other: y_copy(w, c, other, y).start())
        for c in range(C):
            piece = slice(c * part, (c + 1) * part)
            peers(Y, y, lambda other: y_copy(w, c, other, other).wait_recv())
            row_in[w, c, y] = row_out[w, c]
            before = jnp.zeros((part, D), F32)
            for i in range(Y):
                at = i if w == 0 else Y - 1 - i
                grown = jnp.exp(row_in[w, c, at, part : part + 1, :]) * before
                grown = grown + row_in[w, c, at, 0:part, :]
                use = y > at if w == 0 else y < at
                before = jnp.where(use, grown, before)

            def finish(other):
                excl[w, other, piece, :] = (
                    excl[w, other, piece, :] + jnp.exp(fade_d[w, other]) * before
                )

            def leave(other):
                finish(other)
                out_copy(w, c, other, z).start()

            peers(Z, z, leave)
            finish(z)
        state[w, pl.ds(pl.multiple_of(z * rows, rows), rows), :] = excl[w, z]
        for c in range(C):
            peers(Z, z, lambda other: out_copy(w, c, other, other).wait_recv())

    enter(0)

    for h in range(H):
        column = jnp.broadcast_to(cum_col[:, h : h + 1], (T, T))
        growth = jnp.exp(column)
        growth_s[h] = growth
        spread = column - cum_row[h : h + 1, :]
        decay = jnp.where(causal, jnp.exp(jnp.minimum(spread, 0.0)), 0.0)
        decay_s[h] = decay
        weights = (dot(head(q_ref, h), head(k_ref, h), NT) * decay).astype(BF16)
        weights_s[h] = weights
        intra_s[h] = dot(weights, head(v_ref, h), NN)
        scaled = head(q_ref, h).astype(F32) * growth
        high, low = halves(scaled.T)
        sqt_s[h, :, 0:T] = high
        sqt_s[h, :, T : 2 * T] = low

    scan(0)

    squares = jnp.zeros((T, D), F32)
    inner = jnp.zeros((T, D), F32)
    for h in range(H):
        high, low = halves(state[0, h * D : (h + 1) * D, :])
        q_one = head(q_ref, h)
        carried = dot(
            jnp.concatenate([q_one, q_one], axis=1), jnp.concatenate([high, low], axis=0), NN
        )
        raw = growth_s[h] * carried + intra_s[h]
        raw_s[h] = raw
        squares = squares + raw * raw
        inner = inner + raw * head(ct_ref, h).astype(F32)

    def to_row(x):
        column = jnp.sum(x, axis=1, keepdims=True)
        return jnp.sum(jnp.where(eye, column, 0.0), axis=0, keepdims=True)

    def to_column(x):
        return jnp.sum(jnp.where(eye, x, 0.0), axis=1, keepdims=True)

    sums_out[0:1, :] = to_row(squares)
    sums_out[1:2, :] = to_row(inner)
    peers(N, mine, lambda other: x_copy(other, mine).start())
    sums_in[mine] = sums_out[...]
    peers(N, mine, lambda other: x_copy(other, other).wait_recv())
    gathered = sums_in[0]
    for i in range(1, N):
        gathered = gathered + sums_in[i]
    inverse_row = lax.rsqrt(gathered[0:1, :] / width + 1e-06)
    dot_row = inverse_row * gathered[1:2, :] / width
    inverse = jnp.broadcast_to(to_column(inverse_row), (T, D))
    mean_dot = jnp.broadcast_to(to_column(dot_row), (T, D))
    for h in range(H):
        normed = raw_s[h] * inverse
        raw_s[h] = normed
        grad = (inverse * (head(ct_ref, h).astype(F32) - normed * mean_dot)).astype(BF16)
        rg_s[h] = grad
        block[1, h * D : (h + 1) * D, :] = dot(
            sqt_s[h], jnp.concatenate([grad, grad], axis=0), NN
        )

    enter(1)

    for h in range(H):
        columns = slice(h * D, (h + 1) * D)
        att_ref[:, columns] = raw_s[h].astype(BF16)
        grad = rg_s[h]
        high, low = halves(state[0, h * D : (h + 1) * D, :])
        grad_weights = (dot(grad, head(v_ref, h), NT) * decay_s[h]).astype(BF16)
        carried = dot(
            jnp.concatenate([grad, grad], axis=1), jnp.concatenate([high, low], axis=1), NT
        )
        query_total = growth_s[h] * carried + dot(grad_weights, head(k_ref, h), NN)
        qg_ref[:, columns] = query_total.astype(BF16)
        raw_s[h] = dot(grad_weights, head(q_ref, h), TN)
        intra_s[h] = dot(weights_s[h], grad, TN)

    scan(1)

    for h in range(H):
        columns = slice(h * D, (h + 1) * D)
        high, low = halves(state[1, h * D : (h + 1) * D, :])
        v_one = head(v_ref, h)
        k_one = head(k_ref, h)
        key_part = dot(
            jnp.concatenate([v_one, v_one], axis=1), jnp.concatenate([high, low], axis=1), NT
        )
        value_part = dot(
            jnp.concatenate([k_one, k_one], axis=1), jnp.concatenate([high, low], axis=0), NN
        )
        kg_ref[:, columns] = (raw_s[h] + fade_s[h] * key_part).astype(BF16)
        vg_ref[:, columns] = (intra_s[h] + fade_s[h] * value_part).astype(BF16)

    peers(Z, z, lambda other: t_copy(other, 0, other).wait_send())
    for w in range(2):
        for c in range(C):
            peers(Z, z, lambda other: in_copy(w, c, other, other).wait_send())
            peers(Y, y, lambda other: y_copy(w, c, other, other).wait_send())
            peers(Z, z, lambda other: out_copy(w, c, other, other).wait_send())
    peers(N, mine, lambda other: x_copy(other, other).wait_send())


def local(query_rows, key_rows, value_rows, log_decay, cotangent):
    H, T = log_decay.shape
    D = query_rows.shape[1] // H
    length = lax.axis_size("seq")
    N = lax.axis_size("head")
    Z = ROW
    Y = length // Z
    C = CHUNKS
    rows = H * D // Z
    part = rows // C
    vmem = pl.BlockSpec(memory_space=pltpu.VMEM)
    dma = pltpu.SemaphoreType.DMA
    out = jax.ShapeDtypeStruct(query_rows.shape, BF16)
    return pl.pallas_call(
        functools.partial(kernel, Y, Z, N, C),
        out_shape=(out,) * 4,
        in_specs=[vmem] * 5,
        out_specs=(vmem,) * 4,
        scratch_shapes=[
            pltpu.VMEM((2, H * D, D), F32),
            pltpu.VMEM((2, Z, rows, D), F32),
            pltpu.VMEM((2, Z, rows, D), F32),
            pltpu.VMEM((2, H * D, D), F32),
            pltpu.VMEM((H, 1, D), F32),
            pltpu.VMEM((Z, 1, D), F32),
            pltpu.VMEM((2, Z, 1, D), F32),
            pltpu.VMEM((2, C, part + 8, D), F32),
            pltpu.VMEM((2, C, Y, part + 8, D), F32),
            pltpu.VMEM((8, T), F32),
            pltpu.VMEM((N, 8, T), F32),
            pltpu.VMEM((H, T, T), F32),
            pltpu.VMEM((H, T, T), BF16),
            pltpu.VMEM((H, T, D), F32),
            pltpu.VMEM((H, T, D), F32),
            pltpu.VMEM((H, T, D), BF16),
            pltpu.VMEM((H, D, 2 * T), BF16),
            pltpu.VMEM((H, T, D), F32),
            pltpu.VMEM((H, T, D), F32),
            dma((2, C, Z)),
            dma((2, C, Z)),
            dma((2, C, Z)),
            dma((2, C, Z)),
            dma((2, C, Y)),
            dma((2, C, Y)),
            dma((Z,)),
            dma((Z,)),
            dma((N,)),
            dma((N,)),
        ],
        compiler_params=pltpu.CompilerParams(collective_id=0, has_side_effects=True),
    )(query_rows, key_rows, value_rows, log_decay, cotangent)


def solution(mesh):
    return jax.shard_map(
        local,
        mesh=mesh,
        in_specs=(
            P("seq", "head"),
            P("seq", "head"),
            P("seq", "head"),
            P("head", "seq"),
            P("seq", "head"),
        ),
        out_specs=(P("seq", "head"), P("seq", "head"), P("seq", "head"), P("seq", "head")),
        check_vma=False,
    )
```

```python
import functools

import jax
import jax.numpy as jnp
from jax import lax
from jax.experimental import pallas as pl
from jax.experimental.pallas import tpu as pltpu
from jax.sharding import PartitionSpec as P

ROW = 16
CHUNKS = 2
MESH = pl.DeviceIdType.MESH
F32 = jnp.float32
BF16 = jnp.bfloat16


def dot(a, b, dims, precision=None):
    return lax.dot_general(
        a, b, (dims, ((), ())), precision=precision, preferred_element_type=F32
    )


NN = ((1,), (0,))
NT = ((1,), (1,))
TN = ((0,), (0,))


def halves(x):
    high = x.astype(BF16)
    return high, (x - high.astype(F32)).astype(BF16)


def kernel(
    Y,
    Z,
    N,
    C,
    q_ref,
    k_ref,
    v_ref,
    ld_ref,
    ct_ref,
    att_ref,
    qg_ref,
    kg_ref,
    vg_ref,
    block,
    other_s,
    both_s,
    came,
    excl,
    pref,
    ahead,
    state,
    tot_s,
    tot_in,
    two_s,
    two_in,
    fade_d,
    row_out,
    row_in,
    sums_out,
    sums_in,
    decay_s,
    weights_s,
    intra_s,
    raw_s,
    rg_s,
    sqt_s,
    growth_s,
    fade_s,
    p_ssem,
    p_rsem,
    in_ssem,
    in_rsem,
    out_ssem,
    out_rsem,
    f_ssem,
    f_rsem,
    y_ssem,
    y_rsem,
    t_ssem,
    t_rsem,
    two_ssem,
    two_rsem,
    x_ssem,
    x_rsem,
):
    H = ld_ref.shape[0]
    T = ld_ref.shape[1]
    D = q_ref.shape[1] // H
    M = Z // 2
    size = H * D // (2 * C)
    part = size // M
    width = D * H * N
    seq = lax.axis_index("seq")
    mine = lax.axis_index("head")
    y = lax.div(seq, Z)
    z = lax.rem(seq, Z)
    m = lax.div(z, 2)
    b = lax.rem(z, 2)
    partner = z + 1 - 2 * b

    barrier = pltpu.get_barrier_semaphore()

    def far_first(count, i):
        half = count // 2
        return half + jnp.where(lax.rem(i, 2) == 0, lax.div(i, 2), -lax.div(i + 1, 2))

    def peers(count, at, visit):
        def step(i, carry):
            visit(lax.rem(at + far_first(count, i), count))
            return carry

        lax.fori_loop(0, count - 1, step, 0)

    def across(visit, near_first=False):
        def step(i, carry):
            i = M - 1 - i if near_first else i
            reach = 2 * (M // 2 - lax.div(i, 2)) - 1
            offset = jnp.where(lax.rem(i, 2) == 0, reach, Z - reach)
            visit(lax.rem(z + offset, Z))
            return carry

        lax.fori_loop(0, M, step, 0)

    def z_device(other):
        return (y * Z + other, mine)

    def y_device(other):
        return (other * Z + z, mine)

    def x_device(other):
        return (seq, other)

    def greet(device):
        pl.semaphore_signal(barrier, inc=1, device_id=device, device_id_type=MESH)

    across(lambda other: greet(z_device(other)))
    peers(Y, y, lambda other: greet(y_device(other)))
    peers(N, mine, lambda other: greet(x_device(other)))

    t_i = lax.broadcasted_iota(jnp.int32, (T, T), 0)
    s_i = lax.broadcasted_iota(jnp.int32, (T, T), 1)
    causal = t_i >= s_i
    eye = t_i == s_i
    lower = causal.astype(F32)
    ld = ld_ref[...]
    cum_row = dot(ld, lower, NT, lax.Precision.HIGHEST)
    cum_col = dot(lower, ld, NT, lax.Precision.HIGHEST)
    totals = cum_row[:, T - 1 : T]

    def head(ref, h):
        return ref[:, h * D : (h + 1) * D]

    def remote(src, dst, send, recv, device):
        return pltpu.make_async_remote_copy(
            src_ref=src,
            dst_ref=dst,
            send_sem=send,
            recv_sem=recv,
            device_id=device,
            device_id_type=MESH,
        )

    def span(half, c):
        return pl.ds(pl.multiple_of((half * C + c) * size, size), size)

    def strip(slot):
        return pl.ds(pl.multiple_of(slot * part, part), part)

    def t_copy():
        return remote(tot_s, tot_in, t_ssem, t_rsem, z_device(partner))

    def pair_copy(w, c):
        return remote(
            block.at[w, span(1 - b, c)],
            other_s.at[w, c],
            p_ssem.at[w, c],
            p_rsem.at[w, c],
            z_device(partner),
        )

    def two_copy(other, slot):
        at = lax.div(other, 2)
        return remote(
            two_s, two_in.at[slot], two_ssem.at[at], two_rsem.at[slot], z_device(other)
        )

    def in_copy(w, c, other, slot):
        at = lax.div(other, 2)
        return remote(
            both_s.at[w, c, strip(at)],
            came.at[w, c, slot],
            in_ssem.at[w, c, at],
            in_rsem.at[w, c, slot],
            z_device(other),
        )

    def out_copy(w, c, other, slot):
        at = lax.div(other, 2)
        return remote(
            excl.at[w, c, at],
            pref.at[w, c, strip(slot)],
            out_ssem.at[w, c, at],
            out_rsem.at[w, c, slot],
            z_device(other),
        )

    def forward_copy(w, c, half, slot):
        row = pl.multiple_of((half * C + c) * size + slot * part, part)
        return remote(
            ahead.at[w, c, strip(slot)],
            state.at[w, pl.ds(row, part)],
            f_ssem.at[w, c, slot],
            f_rsem.at[w, c, slot],
            z_device(partner),
        )

    def y_copy(w, c, other, slot):
        return remote(
            row_out.at[w, c],
            row_in.at[w, c, slot],
            y_ssem.at[w, c, other],
            y_rsem.at[w, c, slot],
            y_device(other),
        )

    def x_copy(other, slot):
        return remote(
            sums_out, sums_in.at[slot], x_ssem.at[other], x_rsem.at[slot], x_device(other)
        )

    def half_of(other):
        return lax.div(other, 2)

    def enter(w):
        for c in range(C):
            pair_copy(w, c).wait_recv()
            own = block[w, span(b, c), :]
            given = other_s[w, c]
            own_leads = b == w
            lead = jnp.where(own_leads, own, given)
            trail = jnp.where(own_leads, given, own)
            mine_t = tot_s[b * C + c]
            given_t = tot_in[b * C + c]
            trail_t = jnp.where(own_leads, given_t, mine_t)
            both_s[w, c] = jnp.exp(trail_t) * lead + trail
            across(lambda other: in_copy(w, c, other, m).start())

    def scan(w):
        for c in range(C):
            if w == 0 and c == 0:
                across(lambda other: two_copy(other, half_of(other)).wait_recv())
            across(lambda other: in_copy(w, c, other, half_of(other)).wait_recv())

            def step(i, carry):
                total, passed = carry
                at = i if w == 0 else M - 1 - i
                excl[w, c, at] = total
                fade_d[w, c, at] = passed
                one = two_in[at, c]
                total = jnp.exp(one) * total + came[w, c, at]
                return total, passed + one

            total, passed = lax.fori_loop(
                0, M, step, (jnp.zeros((part, D), F32), jnp.zeros((1, D), F32)), unroll=True
            )
            row_out[w, c, 0:part, :] = total
            row_out[w, c, part : part + 8, :] = jnp.broadcast_to(passed, (8, D))
            peers(Y, y, lambda other: y_copy(w, c, other, y).start())
        for c in range(C):
            peers(Y, y, lambda other: y_copy(w, c, other, other).wait_recv())
            row_in[w, c, y] = row_out[w, c]
            before = jnp.zeros((part, D), F32)
            for i in range(Y):
                at = i if w == 0 else Y - 1 - i
                grown = jnp.exp(row_in[w, c, at, part : part + 1, :]) * before
                grown = grown + row_in[w, c, at, 0:part, :]
                use = y > at if w == 0 else y < at
                before = jnp.where(use, grown, before)

            def leave(other):
                at = half_of(other)
                excl[w, c, at] = excl[w, c, at] + jnp.exp(fade_d[w, c, at]) * before
                out_copy(w, c, other, m).start()

            across(leave)
        for c in range(C):
            own_leads = b == w
            mine_t = tot_s[b * C + c]
            given_t = tot_in[b * C + c]
            lead_t = jnp.exp(jnp.where(own_leads, mine_t, given_t))

            def land(other):
                slot = half_of(other)
                out_copy(w, c, other, slot).wait_recv()
                row = pl.multiple_of((b * C + c) * size + slot * part, part)
                own = block[w, pl.ds(row, part), :]
                given = other_s[w, c, strip(slot), :]
                lead = jnp.where(own_leads, own, given)
                first = pref[w, c, strip(slot), :]
                second = lead_t * first + lead
                ahead[w, c, strip(slot), :] = jnp.where(own_leads, second, first)
                forward_copy(w, c, b, slot).start()
                state[w, pl.ds(row, part), :] = jnp.where(own_leads, first, second)

            across(land, near_first=True)
        for c in range(C):
            across(lambda other: forward_copy(w, c, 1 - b, half_of(other)).wait_recv())

    totals = [jnp.broadcast_to(totals[h : h + 1, :], (1, D)) for h in range(H)]
    for h in range(H):
        tot_s[h] = totals[h]
    order = [half * C + c for c in range(C) for half in range(2)]
    for h in order:
        column = cum_col[:, h : h + 1]
        fade = jnp.exp(totals[h] - jnp.broadcast_to(column, (T, D)))
        fade_s[h] = fade
        scaled = (head(k_ref, h).astype(F32) * fade).astype(BF16)
        block[0, h * D : (h + 1) * D, :] = dot(scaled, head(v_ref, h), TN)

    pl.semaphore_wait(barrier, M + (Y - 1) + (N - 1))

    t_copy().start()
    for c in range(C):
        pair_copy(0, c).start()
    t_copy().wait_recv()
    for c in range(C):
        two_s[c] = tot_s[b * C + c] + tot_in[b * C + c]
    across(lambda other: two_copy(other, m).start())
    enter(0)

    for h in range(H):
        column = jnp.broadcast_to(cum_col[:, h : h + 1], (T, T))
        growth = jnp.exp(column)
        growth_s[h] = growth
        spread = column - cum_row[h : h + 1, :]
        decay = jnp.where(causal, jnp.exp(jnp.minimum(spread, 0.0)), 0.0)
        decay_s[h] = decay
        weights = (dot(head(q_ref, h), head(k_ref, h), NT) * decay).astype(BF16)
        weights_s[h] = weights
        intra_s[h] = dot(weights, head(v_ref, h), NN)
        scaled = head(q_ref, h).astype(F32) * growth
        high, low = halves(scaled.T)
        sqt_s[h, :, 0:T] = high
        sqt_s[h, :, T : 2 * T] = low

    scan(0)

    squares = jnp.zeros((T, D), F32)
    inner = jnp.zeros((T, D), F32)
    for h in range(H):
        high, low = halves(state[0, h * D : (h + 1) * D, :])
        q_one = head(q_ref, h)
        carried = dot(
            jnp.concatenate([q_one, q_one], axis=1), jnp.concatenate([high, low], axis=0), NN
        )
        raw = growth_s[h] * carried + intra_s[h]
        raw_s[h] = raw
        squares = squares + raw * raw
        inner = inner + raw * head(ct_ref, h).astype(F32)

    def to_row(x):
        column = jnp.sum(x, axis=1, keepdims=True)
        return jnp.sum(jnp.where(eye, column, 0.0), axis=0, keepdims=True)

    def to_column(x):
        return jnp.sum(jnp.where(eye, x, 0.0), axis=1, keepdims=True)

    sums_out[0:1, :] = to_row(squares)
    sums_out[1:2, :] = to_row(inner)
    peers(N, mine, lambda other: x_copy(other, mine).start())
    sums_in[mine] = sums_out[...]
    peers(N, mine, lambda other: x_copy(other, other).wait_recv())
    gathered = sums_in[0]
    for i in range(1, N):
        gathered = gathered + sums_in[i]
    inverse_row = lax.rsqrt(gathered[0:1, :] / width + 1e-06)
    dot_row = inverse_row * gathered[1:2, :] / width
    inverse = jnp.broadcast_to(to_column(inverse_row), (T, D))
    mean_dot = jnp.broadcast_to(to_column(dot_row), (T, D))
    for c in range(C):
        for h in (c, C + c):
            normed = raw_s[h] * inverse
            raw_s[h] = normed
            grad = (inverse * (head(ct_ref, h).astype(F32) - normed * mean_dot)).astype(BF16)
            rg_s[h] = grad
            block[1, h * D : (h + 1) * D, :] = dot(
                sqt_s[h], jnp.concatenate([grad, grad], axis=0), NN
            )
        pair_copy(1, c).start()

    enter(1)

    for h in range(H):
        columns = slice(h * D, (h + 1) * D)
        att_ref[:, columns] = raw_s[h].astype(BF16)
        grad = rg_s[h]
        high, low = halves(state[0, h * D : (h + 1) * D, :])
        grad_weights = (dot(grad, head(v_ref, h), NT) * decay_s[h]).astype(BF16)
        carried = dot(
            jnp.concatenate([grad, grad], axis=1), jnp.concatenate([high, low], axis=1), NT
        )
        query_total = growth_s[h] * carried + dot(grad_weights, head(k_ref, h), NN)
        qg_ref[:, columns] = query_total.astype(BF16)
        raw_s[h] = dot(grad_weights, head(q_ref, h), TN)
        intra_s[h] = dot(weights_s[h], grad, TN)

    scan(1)

    for h in range(H):
        columns = slice(h * D, (h + 1) * D)
        high, low = halves(state[1, h * D : (h + 1) * D, :])
        v_one = head(v_ref, h)
        k_one = head(k_ref, h)
        key_part = dot(
            jnp.concatenate([v_one, v_one], axis=1), jnp.concatenate([high, low], axis=1), NT
        )
        value_part = dot(
            jnp.concatenate([k_one, k_one], axis=1), jnp.concatenate([high, low], axis=0), NN
        )
        kg_ref[:, columns] = (raw_s[h] + fade_s[h] * key_part).astype(BF16)
        vg_ref[:, columns] = (intra_s[h] + fade_s[h] * value_part).astype(BF16)

    t_copy().wait_send()
    across(lambda other: two_copy(other, m).wait_send())
    for w in range(2):
        for c in range(C):
            pair_copy(w, c).wait_send()
            across(lambda other: in_copy(w, c, other, m).wait_send())
            peers(Y, y, lambda other: y_copy(w, c, other, y).wait_send())
            across(lambda other: out_copy(w, c, other, m).wait_send())
            across(lambda other: forward_copy(w, c, b, half_of(other)).wait_send())
    peers(N, mine, lambda other: x_copy(other, mine).wait_send())


def hand_over(a_ref, b_ref, c_ref, d_ref, a_out, b_out, c_out, d_out):
    a_out[...] = a_ref[...]
    b_out[...] = b_ref[...]
    c_out[...] = c_ref[...]
    d_out[...] = d_ref[...]


def local(query_rows, key_rows, value_rows, log_decay, cotangent):
    H, T = log_decay.shape
    D = query_rows.shape[1] // H
    length = lax.axis_size("seq")
    N = lax.axis_size("head")
    Z = ROW
    Y = length // Z
    C = CHUNKS
    M = Z // 2
    size = H * D // (2 * C)
    part = size // M
    vmem = pl.BlockSpec(memory_space=pltpu.VMEM)
    dma = pltpu.SemaphoreType.DMA
    out = jax.ShapeDtypeStruct(query_rows.shape, BF16)
    results = pl.pallas_call(
        functools.partial(kernel, Y, Z, N, C),
        out_shape=(out,) * 4,
        in_specs=[vmem] * 5,
        out_specs=(vmem,) * 4,
        scratch_shapes=[
            pltpu.VMEM((2, H * D, D), F32),
            pltpu.VMEM((2, C, size, D), F32),
            pltpu.VMEM((2, C, size, D), F32),
            pltpu.VMEM((2, C, M, part, D), F32),
            pltpu.VMEM((2, C, M, part, D), F32),
            pltpu.VMEM((2, C, size, D), F32),
            pltpu.VMEM((2, C, size, D), F32),
            pltpu.VMEM((2, H * D, D), F32),
            pltpu.VMEM((H, 1, D), F32),
            pltpu.VMEM((H, 1, D), F32),
            pltpu.VMEM((C, 1, D), F32),
            pltpu.VMEM((M, C, 1, D), F32),
            pltpu.VMEM((2, C, M, 1, D), F32),
            pltpu.VMEM((2, C, part + 8, D), F32),
            pltpu.VMEM((2, C, Y, part + 8, D), F32),
            pltpu.VMEM((8, T), F32),
            pltpu.VMEM((N, 8, T), F32),
            pltpu.VMEM((H, T, T), F32),
            pltpu.VMEM((H, T, T), BF16),
            pltpu.VMEM((H, T, D), F32),
            pltpu.VMEM((H, T, D), F32),
            pltpu.VMEM((H, T, D), BF16),
            pltpu.VMEM((H, D, 2 * T), BF16),
            pltpu.VMEM((H, T, D), F32),
            pltpu.VMEM((H, T, D), F32),
            dma((2, C)),
            dma((2, C)),
            dma((2, C, M)),
            dma((2, C, M)),
            dma((2, C, M)),
            dma((2, C, M)),
            dma((2, C, M)),
            dma((2, C, M)),
            dma((2, C, Y)),
            dma((2, C, Y)),
            dma,
            dma,
            dma((M,)),
            dma((M,)),
            dma((N,)),
            dma((N,)),
        ],
        compiler_params=pltpu.CompilerParams(collective_id=0, has_side_effects=True),
    )(query_rows, key_rows, value_rows, log_decay, cotangent)
    return pl.pallas_call(
        hand_over,
        out_shape=(out,) * 4,
        in_specs=[vmem] * 4,
        out_specs=(vmem,) * 4,
    )(*results)


def solution(mesh):
    return jax.shard_map(
        local,
        mesh=mesh,
        in_specs=(
            P("seq", "head"),
            P("seq", "head"),
            P("seq", "head"),
            P("head", "seq"),
            P("seq", "head"),
        ),
        out_specs=(P("seq", "head"), P("seq", "head"), P("seq", "head"), P("seq", "head")),
        check_vma=False,
    )
```

```python
import functools

import jax
import jax.numpy as jnp
from jax import lax
from jax.experimental import pallas as pl
from jax.experimental.pallas import tpu as pltpu
from jax.sharding import PartitionSpec as P

ROW = 16
CHUNKS = 2
MESH = pl.DeviceIdType.MESH
F32 = jnp.float32
BF16 = jnp.bfloat16


def dot(a, b, dims, precision=None):
    return lax.dot_general(
        a, b, (dims, ((), ())), precision=precision, preferred_element_type=F32
    )


NN = ((1,), (0,))
NT = ((1,), (1,))
TN = ((0,), (0,))


def halves(x):
    high = x.astype(BF16)
    return high, (x - high.astype(F32)).astype(BF16)


def kernel(
    Y,
    Z,
    N,
    C,
    q_hbm,
    k_hbm,
    v_hbm,
    ld_hbm,
    ct_hbm,
    att_hbm,
    qg_hbm,
    kg_hbm,
    vg_hbm,
    q_ref,
    k_ref,
    v_ref,
    ld_ref,
    ct_ref,
    att_ref,
    qg_ref,
    kg_ref,
    vg_ref,
    load_sem,
    save_sem,
    grad_sem,
    block,
    other_s,
    both_s,
    came,
    excl,
    pref,
    ahead,
    state,
    tot_s,
    tot_in,
    two_s,
    two_in,
    fade_d,
    row_out,
    row_in,
    sums_out,
    sums_in,
    decay_s,
    weights_s,
    intra_s,
    raw_s,
    rg_s,
    sqt_s,
    growth_s,
    fade_s,
    p_ssem,
    p_rsem,
    in_ssem,
    in_rsem,
    out_ssem,
    out_rsem,
    f_ssem,
    f_rsem,
    y_ssem,
    y_rsem,
    t_ssem,
    t_rsem,
    two_ssem,
    two_rsem,
    x_ssem,
    x_rsem,
):
    H = ld_ref.shape[0]
    T = ld_ref.shape[1]
    D = q_ref.shape[1] // H
    M = Z // 2
    size = H * D // (2 * C)
    part = size // M
    width = D * H * N
    seq = lax.axis_index("seq")
    mine = lax.axis_index("head")
    y = lax.div(seq, Z)
    z = lax.rem(seq, Z)
    m = lax.div(z, 2)
    b = lax.rem(z, 2)
    partner = z + 1 - 2 * b

    loads = [
        pltpu.make_async_copy(src, dst, load_sem.at[i])
        for i, (src, dst) in enumerate(
            (
                (ld_hbm, ld_ref),
                (k_hbm, k_ref),
                (v_hbm, v_ref),
                (q_hbm, q_ref),
                (ct_hbm, ct_ref),
            )
        )
    ]
    barrier = pltpu.get_barrier_semaphore()

    def far_first(count, i):
        half = count // 2
        return half + jnp.where(lax.rem(i, 2) == 0, lax.div(i, 2), -lax.div(i + 1, 2))

    def peers(count, at, visit):
        def step(i, carry):
            visit(lax.rem(at + far_first(count, i), count))
            return carry

        lax.fori_loop(0, count - 1, step, 0)

    def across(visit, near_first=False):
        def step(i, carry):
            i = M - 1 - i if near_first else i
            reach = 2 * (M // 2 - lax.div(i, 2)) - 1
            offset = jnp.where(lax.rem(i, 2) == 0, reach, Z - reach)
            visit(lax.rem(z + offset, Z))
            return carry

        lax.fori_loop(0, M, step, 0)

    def later(w, visit):
        def step(i, carry):
            visit(Y - 1 - i if w == 0 else i)
            return carry

        lax.fori_loop(0, Y - 1 - y if w == 0 else y, step, 0)

    def z_device(other):
        return (y * Z + other, mine)

    def y_device(other):
        return (other * Z + z, mine)

    def x_device(other):
        return (seq, other)

    def greet(device):
        pl.semaphore_signal(barrier, inc=1, device_id=device, device_id_type=MESH)

    for load in loads:
        load.start()
    across(lambda other: greet(z_device(other)))
    peers(Y, y, lambda other: greet(y_device(other)))
    peers(N, mine, lambda other: greet(x_device(other)))

    t_i = lax.broadcasted_iota(jnp.int32, (T, T), 0)
    s_i = lax.broadcasted_iota(jnp.int32, (T, T), 1)
    causal = t_i >= s_i
    eye = t_i == s_i
    lower = causal.astype(F32)
    for load in loads[:3]:
        load.wait()
    ld = ld_ref[...]
    cum_row = dot(ld, lower, NT, lax.Precision.HIGHEST)
    cum_col = dot(lower, ld, NT, lax.Precision.HIGHEST)
    totals = cum_row[:, T - 1 : T]

    def head(ref, h):
        return ref[:, h * D : (h + 1) * D]

    def remote(src, dst, send, recv, device):
        return pltpu.make_async_remote_copy(
            src_ref=src,
            dst_ref=dst,
            send_sem=send,
            recv_sem=recv,
            device_id=device,
            device_id_type=MESH,
        )

    def span(half, c):
        return pl.ds(pl.multiple_of((half * C + c) * size, size), size)

    def strip(slot):
        return pl.ds(pl.multiple_of(slot * part, part), part)

    def t_copy():
        return remote(tot_s, tot_in, t_ssem, t_rsem, z_device(partner))

    def pair_copy(w, c):
        return remote(
            block.at[w, span(1 - b, c)],
            other_s.at[w, c],
            p_ssem.at[w, c],
            p_rsem.at[w, c],
            z_device(partner),
        )

    def two_copy(other, slot):
        at = lax.div(other, 2)
        return remote(
            two_s, two_in.at[slot], two_ssem.at[at], two_rsem.at[slot], z_device(other)
        )

    def in_copy(w, c, other, slot):
        at = lax.div(other, 2)
        return remote(
            both_s.at[w, c, strip(at)],
            came.at[w, c, slot],
            in_ssem.at[w, c, at],
            in_rsem.at[w, c, slot],
            z_device(other),
        )

    def out_copy(w, c, other, slot):
        at = lax.div(other, 2)
        return remote(
            excl.at[w, c, at],
            pref.at[w, c, strip(slot)],
            out_ssem.at[w, c, at],
            out_rsem.at[w, c, slot],
            z_device(other),
        )

    def forward_copy(w, c, half, slot):
        row = pl.multiple_of((half * C + c) * size + slot * part, part)
        return remote(
            ahead.at[w, c, strip(slot)],
            state.at[w, pl.ds(row, part)],
            f_ssem.at[w, c, slot],
            f_rsem.at[w, c, slot],
            z_device(partner),
        )

    def y_copy(w, c, other, slot):
        return remote(
            row_out.at[w, c],
            row_in.at[w, c, slot],
            y_ssem.at[w, c, other],
            y_rsem.at[w, c, slot],
            y_device(other),
        )

    def x_copy(other, slot):
        return remote(
            sums_out, sums_in.at[slot], x_ssem.at[other], x_rsem.at[slot], x_device(other)
        )

    def half_of(other):
        return lax.div(other, 2)

    def enter(w):
        for c in range(C):
            pair_copy(w, c).wait_recv()
            own = block[w, span(b, c), :]
            given = other_s[w, c]
            own_leads = b == w
            lead = jnp.where(own_leads, own, given)
            trail = jnp.where(own_leads, given, own)
            mine_t = tot_s[b * C + c]
            given_t = tot_in[b * C + c]
            trail_t = jnp.where(own_leads, given_t, mine_t)
            both_s[w, c] = jnp.exp(trail_t) * lead + trail
            across(lambda other: in_copy(w, c, other, m).start())

    def scan(w, use):
        for c in range(C):
            if w == 0 and c == 0:
                across(lambda other: two_copy(other, half_of(other)).wait_recv())
            across(lambda other: in_copy(w, c, other, half_of(other)).wait_recv())

            def step(i, carry):
                total, passed = carry
                at = i if w == 0 else M - 1 - i
                excl[w, c, at] = total
                fade_d[w, c, at] = passed
                one = two_in[at, c]
                total = jnp.exp(one) * total + came[w, c, at]
                return total, passed + one

            total, passed = lax.fori_loop(
                0, M, step, (jnp.zeros((part, D), F32), jnp.zeros((1, D), F32)), unroll=True
            )
            row_out[w, c, 0:part, :] = total
            row_out[w, c, part : part + 8, :] = jnp.broadcast_to(passed, (8, D))
            later(w, lambda other: y_copy(w, c, other, y).start())
        for c in range(C):

            def gain(i, before):
                at = i if w == 0 else Y - 1 - i
                y_copy(w, c, at, at).wait_recv()
                grown = jnp.exp(row_in[w, c, at, part : part + 1, :]) * before
                return grown + row_in[w, c, at, 0:part, :]

            before = lax.fori_loop(
                0, y if w == 0 else Y - 1 - y, gain, jnp.zeros((part, D), F32)
            )

            def leave(other):
                at = half_of(other)
                excl[w, c, at] = excl[w, c, at] + jnp.exp(fade_d[w, c, at]) * before
                out_copy(w, c, other, m).start()

            across(leave)
        for c in range(C):
            own_leads = b == w
            mine_t = tot_s[b * C + c]
            given_t = tot_in[b * C + c]
            lead_t = jnp.exp(jnp.where(own_leads, mine_t, given_t))

            def land(other):
                slot = half_of(other)
                out_copy(w, c, other, slot).wait_recv()
                row = pl.multiple_of((b * C + c) * size + slot * part, part)
                own = block[w, pl.ds(row, part), :]
                given = other_s[w, c, strip(slot), :]
                lead = jnp.where(own_leads, own, given)
                first = pref[w, c, strip(slot), :]
                second = lead_t * first + lead
                ahead[w, c, strip(slot), :] = jnp.where(own_leads, second, first)
                forward_copy(w, c, b, slot).start()
                state[w, pl.ds(row, part), :] = jnp.where(own_leads, first, second)

            across(land, near_first=True)
        for c in range(C):
            across(lambda other: forward_copy(w, c, 1 - b, half_of(other)).wait_recv())
            for h in (c, C + c):
                use(h)

    totals = [jnp.broadcast_to(totals[h : h + 1, :], (1, D)) for h in range(H)]
    for h in range(H):
        tot_s[h] = totals[h]
    order = [half * C + c for c in range(C) for half in range(2)]
    for h in order:
        column = cum_col[:, h : h + 1]
        fade = jnp.exp(totals[h] - jnp.broadcast_to(column, (T, D)))
        fade_s[h] = fade
        scaled = (head(k_ref, h).astype(F32) * fade).astype(BF16)
        block[0, h * D : (h + 1) * D, :] = dot(scaled, head(v_ref, h), TN)

    pl.semaphore_wait(barrier, M + (Y - 1) + (N - 1))

    t_copy().start()
    for c in range(C):
        pair_copy(0, c).start()
    t_copy().wait_recv()
    for c in range(C):
        two_s[c] = tot_s[b * C + c] + tot_in[b * C + c]
    across(lambda other: two_copy(other, m).start())
    enter(0)

    for load in loads[3:]:
        load.wait()
    for h in range(H):
        column = jnp.broadcast_to(cum_col[:, h : h + 1], (T, T))
        growth = jnp.exp(column)
        growth_s[h] = growth
        spread = column - cum_row[h : h + 1, :]
        decay = jnp.where(causal, jnp.exp(jnp.minimum(spread, 0.0)), 0.0)
        decay_s[h] = decay
        weights = (dot(head(q_ref, h), head(k_ref, h), NT) * decay).astype(BF16)
        weights_s[h] = weights
        intra_s[h] = dot(weights, head(v_ref, h), NN)
        scaled = head(q_ref, h).astype(F32) * growth
        high, low = halves(scaled.T)
        sqt_s[h, :, 0:T] = high
        sqt_s[h, :, T : 2 * T] = low

    squares = []
    inner = []

    def output(h):
        high, low = halves(state[0, h * D : (h + 1) * D, :])
        q_one = head(q_ref, h)
        carried = dot(
            jnp.concatenate([q_one, q_one], axis=1), jnp.concatenate([high, low], axis=0), NN
        )
        raw = growth_s[h] * carried + intra_s[h]
        raw_s[h] = raw
        squares.append(raw * raw)
        inner.append(raw * head(ct_ref, h).astype(F32))

    scan(0, output)

    def to_row(x):
        column = jnp.sum(x, axis=1, keepdims=True)
        return jnp.sum(jnp.where(eye, column, 0.0), axis=0, keepdims=True)

    def to_column(x):
        return jnp.sum(jnp.where(eye, x, 0.0), axis=1, keepdims=True)

    sums_out[0:1, :] = to_row(sum(squares[1:], squares[0]))
    sums_out[1:2, :] = to_row(sum(inner[1:], inner[0]))
    peers(N, mine, lambda other: x_copy(other, mine).start())
    sums_in[mine] = sums_out[...]
    peers(N, mine, lambda other: x_copy(other, other).wait_recv())
    gathered = sums_in[0]
    for i in range(1, N):
        gathered = gathered + sums_in[i]
    inverse_row = lax.rsqrt(gathered[0:1, :] / width + 1e-06)
    dot_row = inverse_row * gathered[1:2, :] / width
    inverse = jnp.broadcast_to(to_column(inverse_row), (T, D))
    mean_dot = jnp.broadcast_to(to_column(dot_row), (T, D))
    for c in range(C):
        for h in (c, C + c):
            normed = raw_s[h] * inverse
            raw_s[h] = normed
            grad = (inverse * (head(ct_ref, h).astype(F32) - normed * mean_dot)).astype(BF16)
            rg_s[h] = grad
            block[1, h * D : (h + 1) * D, :] = dot(
                sqt_s[h], jnp.concatenate([grad, grad], axis=0), NN
            )
        pair_copy(1, c).start()

    enter(1)

    for h in range(H):
        columns = slice(h * D, (h + 1) * D)
        att_ref[:, columns] = raw_s[h].astype(BF16)
        grad = rg_s[h]
        high, low = halves(state[0, h * D : (h + 1) * D, :])
        grad_weights = (dot(grad, head(v_ref, h), NT) * decay_s[h]).astype(BF16)
        carried = dot(
            jnp.concatenate([grad, grad], axis=1), jnp.concatenate([high, low], axis=1), NT
        )
        query_total = growth_s[h] * carried + dot(grad_weights, head(k_ref, h), NN)
        qg_ref[:, columns] = query_total.astype(BF16)
        raw_s[h] = dot(grad_weights, head(q_ref, h), TN)
        intra_s[h] = dot(weights_s[h], grad, TN)

    saves = [
        pltpu.make_async_copy(att_ref, att_hbm, save_sem.at[0]),
        pltpu.make_async_copy(qg_ref, qg_hbm, save_sem.at[1]),
    ]
    for save in saves:
        save.start()

    def gradients(h):
        columns = slice(h * D, (h + 1) * D)
        high, low = halves(state[1, h * D : (h + 1) * D, :])
        v_one = head(v_ref, h)
        k_one = head(k_ref, h)
        key_part = dot(
            jnp.concatenate([v_one, v_one], axis=1), jnp.concatenate([high, low], axis=1), NT
        )
        value_part = dot(
            jnp.concatenate([k_one, k_one], axis=1), jnp.concatenate([high, low], axis=0), NN
        )
        kg_ref[:, columns] = (raw_s[h] + fade_s[h] * key_part).astype(BF16)
        vg_ref[:, columns] = (intra_s[h] + fade_s[h] * value_part).astype(BF16)
        for i, (src, dst) in enumerate(((kg_ref, kg_hbm), (vg_ref, vg_hbm))):
            save = pltpu.make_async_copy(
                src.at[:, columns], dst.at[:, columns], grad_sem.at[i, h]
            )
            save.start()
            saves.append(save)

    scan(1, gradients)

    t_copy().wait_send()
    across(lambda other: two_copy(other, m).wait_send())
    for w in range(2):
        for c in range(C):
            pair_copy(w, c).wait_send()
            across(lambda other: in_copy(w, c, other, m).wait_send())
            later(w, lambda other: y_copy(w, c, other, y).wait_send())
            across(lambda other: out_copy(w, c, other, m).wait_send())
            across(lambda other: forward_copy(w, c, b, half_of(other)).wait_send())
    peers(N, mine, lambda other: x_copy(other, mine).wait_send())
    for save in saves:
        save.wait()


def hand_over(*refs):
    sources, targets, held = refs[0:4], refs[4:8], refs[8:12]
    load_sem, save_sem = refs[12:14]
    loads = [
        pltpu.make_async_copy(src, dst, load_sem.at[i])
        for i, (src, dst) in enumerate(zip(sources, held))
    ]
    saves = [
        pltpu.make_async_copy(src, dst, save_sem.at[i])
        for i, (src, dst) in enumerate(zip(held, targets))
    ]
    for load in loads:
        load.start()
    for load, save in zip(loads, saves):
        load.wait()
        save.start()
    for save in saves:
        save.wait()


def local(query_rows, key_rows, value_rows, log_decay, cotangent):
    H, T = log_decay.shape
    D = query_rows.shape[1] // H
    length = lax.axis_size("seq")
    N = lax.axis_size("head")
    Z = ROW
    Y = length // Z
    C = CHUNKS
    M = Z // 2
    size = H * D // (2 * C)
    part = size // M
    anywhere = pl.BlockSpec(memory_space=pl.ANY)
    dma = pltpu.SemaphoreType.DMA
    out = jax.ShapeDtypeStruct(query_rows.shape, BF16)
    results = pl.pallas_call(
        functools.partial(kernel, Y, Z, N, C),
        out_shape=(out,) * 4,
        in_specs=[anywhere] * 5,
        out_specs=(anywhere,) * 4,
        scratch_shapes=[
            pltpu.VMEM((T, H * D), BF16),
            pltpu.VMEM((T, H * D), BF16),
            pltpu.VMEM((T, H * D), BF16),
            pltpu.VMEM((H, T), F32),
            pltpu.VMEM((T, H * D), BF16),
            pltpu.VMEM((T, H * D), BF16),
            pltpu.VMEM((T, H * D), BF16),
            pltpu.VMEM((T, H * D), BF16),
            pltpu.VMEM((T, H * D), BF16),
            dma((5,)),
            dma((2,)),
            dma((2, H)),
            pltpu.VMEM((2, H * D, D), F32),
            pltpu.VMEM((2, C, size, D), F32),
            pltpu.VMEM((2, C, size, D), F32),
            pltpu.VMEM((2, C, M, part, D), F32),
            pltpu.VMEM((2, C, M, part, D), F32),
            pltpu.VMEM((2, C, size, D), F32),
            pltpu.VMEM((2, C, size, D), F32),
            pltpu.VMEM((2, H * D, D), F32),
            pltpu.VMEM((H, 1, D), F32),
            pltpu.VMEM((H, 1, D), F32),
            pltpu.VMEM((C, 1, D), F32),
            pltpu.VMEM((M, C, 1, D), F32),
            pltpu.VMEM((2, C, M, 1, D), F32),
            pltpu.VMEM((2, C, part + 8, D), F32),
            pltpu.VMEM((2, C, Y, part + 8, D), F32),
            pltpu.VMEM((8, T), F32),
            pltpu.VMEM((N, 8, T), F32),
            pltpu.VMEM((H, T, T), F32),
            pltpu.VMEM((H, T, T), BF16),
            pltpu.VMEM((H, T, D), F32),
            pltpu.VMEM((H, T, D), F32),
            pltpu.VMEM((H, T, D), BF16),
            pltpu.VMEM((H, D, 2 * T), BF16),
            pltpu.VMEM((H, T, D), F32),
            pltpu.VMEM((H, T, D), F32),
            dma((2, C)),
            dma((2, C)),
            dma((2, C, M)),
            dma((2, C, M)),
            dma((2, C, M)),
            dma((2, C, M)),
            dma((2, C, M)),
            dma((2, C, M)),
            dma((2, C, Y)),
            dma((2, C, Y)),
            dma,
            dma,
            dma((M,)),
            dma((M,)),
            dma((N,)),
            dma((N,)),
        ],
        compiler_params=pltpu.CompilerParams(collective_id=0, has_side_effects=True),
    )(query_rows, key_rows, value_rows, log_decay, cotangent)
    return pl.pallas_call(
        hand_over,
        out_shape=(out,) * 4,
        in_specs=[anywhere] * 4,
        out_specs=(anywhere,) * 4,
        scratch_shapes=[pltpu.VMEM((T, H * D), BF16)] * 4 + [dma((4,)), dma((4,))],
    )(*results)


def solution(mesh):
    return jax.shard_map(
        local,
        mesh=mesh,
        in_specs=(
            P("seq", "head"),
            P("seq", "head"),
            P("seq", "head"),
            P("head", "seq"),
            P("seq", "head"),
        ),
        out_specs=(P("seq", "head"), P("seq", "head"), P("seq", "head"), P("seq", "head")),
        check_vma=False,
    )
```
